1024 devices in a mesh: row: 16 (over y, core), col: 64 (over z, x).
Axes of the slice: x: 4, y: 8, z: 16, core: 2. Of those that a mesh axis runs over, the one named last changes fastest.
Arguments:
- tokens: bfloat16 [1024, 8192], P('col', 'row'), may hold values from -120 to 120
- source: int32 [1024], replicated, may hold values from 0 to 1023, each once
- gain: float32 [8192], P('row'), may hold values from 0.5 to 1.5
- gate_weight: bfloat16 [8192, 29568], P('row', 'col'), may hold values from -0.0625 to 0.0625
- up_weight: bfloat16 [8192, 29568], P('row', 'col'), may hold values from -0.0625 to 0.0625
- down_weight: bfloat16 [29568, 8192], P('col', 'row'), may hold values from -0.03125 to 0.03125
Outputs:
- mixed: bfloat16 [1024, 8192], P('col', 'row')
The draws below stay inside these ranges and needn't reach their ends.
All inputs are finite; a program needn't handle non-finite values.
Results may differ from the reference program's by a relative error of at most 0.0064.
Values may be sent and summed in bfloat16 or wider, within the bound.
No kernel may reach another device: no remote copies, remote signals or barrier semaphores. Data moves between devices by JAX's collectives and lax.ppermute only.
A program may use at most 32 MiB of HBM per device.

```python
import jax
import jax.numpy as jnp
from jax import lax

D = 8192
FF = 29568
TOKENS = 1024


def draw_tokens(key, part):
    first, second = jax.random.split(key, 2)
    position = jnp.arange(D, dtype=jnp.float32) / D
    column_scale = 10.0 ** position
    row_scale = 10.0 ** jax.random.uniform(first, (TOKENS, 1), dtype=jnp.float32)
    values = jnp.clip(jax.random.normal(second, (TOKENS, D), dtype=jnp.float32), -4.0, 4.0)
    return (0.3 * values * column_scale * row_scale).astype(jnp.bfloat16)


def shard_levels(own_key, extent, pieces, low, largest):
    def one(dim, blocks):
        draws = jax.random.uniform(jax.random.fold_in(jax.random.fold_in(own_key, 6), dim), (blocks,), jnp.float32, low / len(pieces), largest / len(pieces))
        return jnp.repeat(jnp.exp(draws), extent[dim] // blocks).reshape((-1,) + (1,) * (len(extent) - dim - 1))

    loudness = one(*pieces[0])
    for cut in pieces[1:]:
        loudness = loudness * one(*cut)
    return loudness


def scatter_about(stream_key, extent, scale, limit, pieces=(), kind=jnp.bfloat16):
    factor_of = shard_levels(stream_key, extent, pieces, -0.22, 0.18) if pieces else 1.0
    result = jax.random.normal(stream_key, extent, jnp.float32) * scale * factor_of
    return jnp.minimum(jnp.maximum(result, -limit), limit).astype(kind)


def setup_inputs(seed: int = 0) -> dict:
    keys = jax.random.split(jax.random.key(seed), 7)
    tokens = draw_tokens(jax.random.fold_in(keys[6], 71), 0)
    source = jax.random.permutation(keys[1], TOKENS).astype(jnp.int32)
    gain = jnp.clip(0.5 + 1.0 * jax.random.uniform(keys[2], (D,), jnp.float32) ** shard_levels(keys[2], (D,), ((0, 16),), -0.2, 0.2), 0.5, 1.5)
    gate_weight = scatter_about(keys[3], (D, FF), D ** -0.5, 0.0625, ((0, 16), (1, 64)))
    up_weight = scatter_about(keys[4], (D, FF), D ** -0.5, 0.0625, ((0, 16), (1, 64)))
    down_weight = scatter_about(keys[5], (FF, D), FF ** -0.5, 0.03125, ((0, 64), (1, 16)))
    return {"tokens": tokens, "source": source, "gain": gain, "gate_weight": gate_weight, "up_weight": up_weight, "down_weight": down_weight}


def reference(tokens, source, gain, gate_weight, up_weight, down_weight):
    merged = jnp.take(tokens, source, axis=0)
    wide = merged.astype(jnp.float32)
    squares = lax.optimization_barrier(jnp.sum(wide * wide, axis=1, keepdims=True))
    scale = lax.rsqrt(squares / D + 1e-06)
    weighted = (wide * gain).astype(jnp.bfloat16)
    gate = scale * jnp.dot(weighted, gate_weight, preferred_element_type=jnp.float32)
    up = scale * jnp.dot(weighted, up_weight, preferred_element_type=jnp.float32)
    hidden = (jax.nn.silu(gate) * up).astype(jnp.bfloat16)
    return jnp.dot(hidden, down_weight, preferred_element_type=jnp.float32).astype(jnp.bfloat16)
```

```python
import functools

import jax
import jax.numpy as jnp
from jax import lax
from jax.experimental import pallas as pl
from jax.experimental.pallas import tpu as pltpu
from jax.sharding import Mesh
from jax.sharding import PartitionSpec as P

WIDTH = 8192
INTERPRET = False
NT = (((1,), (1,)), ((), ()))


def swapped(value, axis):
    return lax.all_to_all(value, axis, split_axis=0, concat_axis=0, tiled=True)


def copied_to_all(value, axis):
    copies = jnp.broadcast_to(value, (lax.axis_size(axis), *value.shape))
    return swapped(copies, axis).reshape(-1, *value.shape[1:])


def summed(pieces):
    return jnp.sum(pieces.astype(jnp.float32), axis=0).astype(jnp.bfloat16)


def products_kernel(sizes, other, source_ref, gathered_ref, gain_ref, gate_ref, up_ref, out_ref, pick_ref, weight_ref):
    ny, nc, nz, nx, share = sizes
    total = gathered_ref.shape[0]
    units, half = gate_ref.shape[0], weight_ref.shape[0]
    block = total // (ny * nc)
    core = lax.axis_index("c")
    wanted = nc - 1 - core if other else core
    row = lax.broadcasted_iota(jnp.int32, (share, total), 1)
    token = ((row // share % nz) * nx + row // (share * nz)) * share + row % share
    for y in range(ny):
        for k in range(block // share):
            starts = []
            for c in range(nc):
                q = (y * nc + c) * block // share + k
                starts.append((q % nz * nx + q // nz) * share)
            start = pl.multiple_of(jnp.where(wanted == 0, starts[0], starts[1]), share)
            ids = source_ref[pl.ds(start, share), :]
            at = y * block + k * share
            pick_ref[at : at + share, :] = jnp.where(ids == token, 1.0, 0.0).astype(jnp.bfloat16)
    merged = jnp.dot(pick_ref[...], gathered_ref[...], preferred_element_type=jnp.float32)
    squares = jnp.sum(merged * merged, axis=1, keepdims=True)
    weighted = (merged * gain_ref[...]).astype(jnp.bfloat16)
    weight_ref[units:, :] = jnp.zeros((half - units, weight_ref.shape[1]), jnp.bfloat16)
    weight_ref[:units, :] = gate_ref[...]
    gate = lax.dot_general(weighted, weight_ref[...], NT, preferred_element_type=jnp.float32)
    lane = lax.broadcasted_iota(jnp.int32, gate.shape, 1)
    out_ref[:, :half] = jnp.where(lane == units, squares, gate).astype(out_ref.dtype)
    weight_ref[:units, :] = up_ref[...]
    up = lax.dot_general(weighted, weight_ref[...], NT, preferred_element_type=jnp.float32)
    out_ref[:, half:] = up.astype(out_ref.dtype)


def products(sizes, other, kind, source, gathered, gain, gate_weight, up_weight):
    units, depth = gate_weight.shape
    half = -(-(units + 1) // 128) * 128
    kept = gathered.shape[0] // sizes[1]
    return pl.pallas_call(
        functools.partial(products_kernel, sizes, other),
        out_shape=jax.ShapeDtypeStruct((kept, 2 * half), kind),
        scratch_shapes=[
            pltpu.VMEM((kept, gathered.shape[0]), jnp.bfloat16),
            pltpu.VMEM((half, depth), jnp.bfloat16),
        ],
        interpret=INTERPRET,
        name="products_other" if other else "products_own",
    )(source, gathered, gain, gate_weight, up_weight)


def activate_kernel(units, pieces_ref, out_ref):
    total = jnp.sum(pieces_ref[...].astype(jnp.float32), axis=0)
    half = total.shape[1] // 2
    gate, up = total[:, :half], total[:, half:]
    scale = lax.rsqrt(gate[:, units : units + 1] / WIDTH + 1e-6)
    gate, up = scale * gate[:, :units], scale * up[:, :units]
    out_ref[...] = (gate / (1.0 + jnp.exp(-gate)) * up).astype(jnp.bfloat16)


def activate(pieces, units):
    return pl.pallas_call(
        functools.partial(activate_kernel, units),
        out_shape=jax.ShapeDtypeStruct((pieces.shape[1], units), jnp.bfloat16),
        interpret=INTERPRET,
        name="activate",
    )(pieces)


def on_device(tokens, source, gain, gate_weight, up_weight, down_weight):
    ny, nc, nz, nx = (lax.axis_size(a) for a in ("y", "c", "z", "x"))
    share, depth = tokens.shape
    sizes = (ny, nc, nz, nx, share)
    units = gate_weight.shape[1]
    gathered = copied_to_all(copied_to_all(tokens, "z"), "x")
    operands = (source[:, None], gathered, gain[None, :], gate_weight.T, up_weight.T)
    given = products(sizes, True, jnp.bfloat16, *operands)
    taken = lax.ppermute(given, "c", [(0, 1), (1, 0)])
    own = products(sizes, False, jnp.float32, *operands)
    both = (own + taken.astype(jnp.float32)).astype(jnp.bfloat16)
    pieces = swapped(both.reshape(ny, -1, both.shape[1]), "y")
    hidden = lax.all_gather(activate(pieces, units), ("y", "c"), axis=0, tiled=True)
    mixed = jnp.dot(hidden, down_weight, preferred_element_type=jnp.float32).astype(jnp.bfloat16)
    mixed = summed(swapped(mixed.reshape(nx, -1, depth), "x"))
    return summed(swapped(mixed.reshape(nz, share, depth), "z"))


def solution(mesh):
    row, col = mesh.shape["row"], mesh.shape["col"]
    finer = Mesh(mesh.devices.reshape(row // 2, 2, col // 4, 4), ("y", "c", "z", "x"))
    rows, cols = ("y", "c"), ("z", "x")
    placed = (P(cols, rows), P(), P(rows), P(rows, cols), P(rows, cols), P(cols, rows))
    return jax.shard_map(
        on_device, mesh=finer, in_specs=placed, out_specs=P(cols, rows), check_vma=False
    )
```

```python
import functools

import jax
import jax.numpy as jnp
from jax import lax
from jax.experimental import pallas as pl
from jax.experimental.pallas import tpu as pltpu
from jax.sharding import Mesh
from jax.sharding import PartitionSpec as P

WIDTH = 8192
VM = pl.BlockSpec(memory_space=pltpu.VMEM)
INTERPRET = False
NT = (((1,), (1,)), ((), ()))


def swapped(value, axis):
    return lax.all_to_all(value, axis, split_axis=0, concat_axis=0, tiled=True)


def copied_to_all(value, axis):
    copies = jnp.broadcast_to(value, (lax.axis_size(axis), *value.shape))
    return swapped(copies, axis).reshape(-1, *value.shape[1:])


def summed(pieces):
    return jnp.sum(pieces.astype(jnp.float32), axis=0).astype(jnp.bfloat16)


def products_kernel(sizes, other, source_ref, gathered_ref, gain_ref, gate_ref, up_ref, out_ref, pick_ref, weight_ref):
    ny, nc, nz, nx, share = sizes
    total = gathered_ref.shape[0]
    units, half = gate_ref.shape[0], weight_ref.shape[0]
    block = total // (ny * nc)
    core = lax.axis_index("c")
    wanted = nc - 1 - core if other else core
    row = lax.broadcasted_iota(jnp.int32, (share, total), 1)
    token = ((row // share % nz) * nx + row // (share * nz)) * share + row % share
    for y in range(ny):
        for k in range(block // share):
            starts = []
            for c in range(nc):
                q = (y * nc + c) * block // share + k
                starts.append((q % nz * nx + q // nz) * share)
            start = pl.multiple_of(jnp.where(wanted == 0, starts[0], starts[1]), share)
            ids = source_ref[pl.ds(start, share), :]
            at = y * block + k * share
            pick_ref[at : at + share, :] = jnp.where(ids == token, 1.0, 0.0).astype(jnp.bfloat16)
    merged = jnp.dot(pick_ref[...], gathered_ref[...], preferred_element_type=jnp.float32)
    squares = jnp.sum(merged * merged, axis=1, keepdims=True)
    weighted = (merged * gain_ref[...]).astype(jnp.bfloat16)
    weight_ref[units:, :] = jnp.zeros((half - units, weight_ref.shape[1]), jnp.bfloat16)
    weight_ref[:units, :] = gate_ref[...]
    gate = lax.dot_general(weighted, weight_ref[...], NT, preferred_element_type=jnp.float32)
    lane = lax.broadcasted_iota(jnp.int32, gate.shape, 1)
    out_ref[:, :half] = jnp.where(lane == units, squares, gate).astype(out_ref.dtype)
    weight_ref[:units, :] = up_ref[...]
    up = lax.dot_general(weighted, weight_ref[...], NT, preferred_element_type=jnp.float32)
    out_ref[:, half:] = up.astype(out_ref.dtype)


def products(sizes, other, kind, source, gathered, gain, gate_weight, up_weight):
    units, depth = gate_weight.shape
    half = -(-(units + 1) // 128) * 128
    kept = gathered.shape[0] // sizes[1]
    return pl.pallas_call(
        functools.partial(products_kernel, sizes, other),
        out_shape=jax.ShapeDtypeStruct((kept, 2 * half), kind),
        scratch_shapes=[
            pltpu.VMEM((kept, gathered.shape[0]), jnp.bfloat16),
            pltpu.VMEM((half, depth), jnp.bfloat16),
        ],
        interpret=INTERPRET, compiler_params=pltpu.CompilerParams(vmem_limit_bytes=16 << 20), in_specs=[VM] * 5, out_specs=VM,
        name="products_other" if other else "products_own",
    )(source, gathered, gain, gate_weight, up_weight)


def activate_kernel(units, pieces_ref, out_ref):
    total = jnp.sum(pieces_ref[...].astype(jnp.float32), axis=0)
    half = total.shape[1] // 2
    gate, up = total[:, :half], total[:, half:]
    scale = lax.rsqrt(gate[:, units : units + 1] / WIDTH + 1e-6)
    gate, up = scale * gate[:, :units], scale * up[:, :units]
    out_ref[...] = (gate / (1.0 + jnp.exp(-gate)) * up).astype(jnp.bfloat16)


def activate(pieces, units):
    return pl.pallas_call(
        functools.partial(activate_kernel, units),
        out_shape=jax.ShapeDtypeStruct((pieces.shape[1], units), jnp.bfloat16),
        interpret=INTERPRET, compiler_params=pltpu.CompilerParams(vmem_limit_bytes=16 << 20), in_specs=[VM], out_specs=VM,
        name="activate",
    )(pieces)


def on_device(tokens, source, gain, gate_weight, up_weight, down_weight):
    ny, nc, nz, nx = (lax.axis_size(a) for a in ("y", "c", "z", "x"))
    share, depth = tokens.shape
    sizes = (ny, nc, nz, nx, share)
    units = gate_weight.shape[1]
    gathered = copied_to_all(copied_to_all(tokens, "z"), "x")
    operands = (source[:, None], gathered, gain[None, :], gate_weight.T, up_weight.T)
    given = products(sizes, True, jnp.bfloat16, *operands)
    taken = lax.ppermute(given, "c", [(0, 1), (1, 0)])
    own = products(sizes, False, jnp.float32, *operands)
    both = (own + taken.astype(jnp.float32)).astype(jnp.bfloat16)
    pieces = swapped(both.reshape(ny, -1, both.shape[1]), "y")
    hidden = lax.all_gather(activate(pieces, units), ("y", "c"), axis=0, tiled=True)
    mixed = jnp.dot(hidden, down_weight, preferred_element_type=jnp.float32).astype(jnp.bfloat16)
    mixed = summed(swapped(mixed.reshape(nx, -1, depth), "x"))
    return summed(swapped(mixed.reshape(nz, share, depth), "z"))


def solution(mesh):
    row, col = mesh.shape["row"], mesh.shape["col"]
    finer = Mesh(mesh.devices.reshape(row // 2, 2, col // 4, 4), ("y", "c", "z", "x"))
    rows, cols = ("y", "c"), ("z", "x")
    placed = (P(cols, rows), P(), P(rows), P(rows, cols), P(rows, cols), P(cols, rows))
    return jax.shard_map(
        on_device, mesh=finer, in_specs=placed, out_specs=P(cols, rows), check_vma=False
    )
```

```python
import functools

import jax
import jax.numpy as jnp
from jax import lax
from jax.experimental import pallas as pl
from jax.experimental.pallas import tpu as pltpu
from jax.sharding import Mesh
from jax.sharding import PartitionSpec as P

WIDTH = 8192
X, L = 4, 2
VM = pl.BlockSpec(memory_space=pltpu.VMEM)
INTERPRET = False
NEAR = ("l", "x")
NT = (((1,), (1,)), ((), ()))


def swapped(value, axis):
    return lax.all_to_all(value, axis, split_axis=0, concat_axis=0, tiled=True)


def copied_to_all(value, axis):
    copies = jnp.broadcast_to(value, (lax.axis_size(axis), *value.shape))
    return swapped(copies, axis).reshape(-1, *value.shape[1:])


def summed(pieces):
    return jnp.sum(pieces.astype(jnp.float32), axis=0).astype(jnp.bfloat16)


def products_kernel(sizes, other, source_ref, gathered_ref, gain_ref, gate_ref, up_ref, out_ref, pick_ref, weight_ref):
    ny, nc, nh, nl, nx, share = sizes

    def place(n):
        return (n % nh * nl + n // (nh * nx)) * nx + n // nh % nx

    total = gathered_ref.shape[0]
    units, half = gate_ref.shape[0], weight_ref.shape[0]
    block = total // (ny * nc)
    core = lax.axis_index("c")
    wanted = nc - 1 - core if other else core
    row = lax.broadcasted_iota(jnp.int32, (share, total), 1)
    token = place(row // share) * share + row % share
    for y in range(ny):
        for k in range(block // share):
            starts = [place((y * nc + c) * block // share + k) * share for c in range(nc)]
            start = pl.multiple_of(jnp.where(wanted == 0, starts[0], starts[1]), share)
            ids = source_ref[pl.ds(start, share), :]
            at = y * block + k * share
            pick_ref[at : at + share, :] = jnp.where(ids == token, 1.0, 0.0).astype(jnp.bfloat16)
    merged = jnp.dot(pick_ref[...], gathered_ref[...], preferred_element_type=jnp.float32)
    squares = jnp.sum(merged * merged, axis=1, keepdims=True)
    weighted = (merged * gain_ref[...]).astype(jnp.bfloat16)
    weight_ref[units:, :] = jnp.zeros((half - units, weight_ref.shape[1]), jnp.bfloat16)
    weight_ref[:units, :] = gate_ref[...]
    gate = lax.dot_general(weighted, weight_ref[...], NT, preferred_element_type=jnp.float32)
    lane = lax.broadcasted_iota(jnp.int32, gate.shape, 1)
    out_ref[:, :half] = jnp.where(lane == units, squares, gate).astype(out_ref.dtype)
    weight_ref[:units, :] = up_ref[...]
    up = lax.dot_general(weighted, weight_ref[...], NT, preferred_element_type=jnp.float32)
    out_ref[:, half:] = up.astype(out_ref.dtype)


def products(sizes, other, kind, source, gathered, gain, gate_weight, up_weight):
    units, depth = gate_weight.shape
    half = -(-(units + 1) // 128) * 128
    kept = gathered.shape[0] // sizes[1]
    return pl.pallas_call(
        functools.partial(products_kernel, sizes, other),
        out_shape=jax.ShapeDtypeStruct((kept, 2 * half), kind),
        scratch_shapes=[
            pltpu.VMEM((kept, gathered.shape[0]), jnp.bfloat16),
            pltpu.VMEM((half, depth), jnp.bfloat16),
        ],
        interpret=INTERPRET, compiler_params=pltpu.CompilerParams(vmem_limit_bytes=16 << 20), in_specs=[VM] * 5, out_specs=VM,
        name="products_other" if other else "products_own",
    )(source, gathered, gain, gate_weight, up_weight)


def activate_kernel(units, pieces_ref, out_ref):
    total = jnp.sum(pieces_ref[...].astype(jnp.float32), axis=0)
    half = total.shape[1] // 2
    gate, up = total[:, :half], total[:, half:]
    scale = lax.rsqrt(gate[:, units : units + 1] / WIDTH + 1e-6)
    gate, up = scale * gate[:, :units], scale * up[:, :units]
    out_ref[...] = (gate / (1.0 + jnp.exp(-gate)) * up).astype(jnp.bfloat16)


def activate(pieces, units):
    return pl.pallas_call(
        functools.partial(activate_kernel, units),
        out_shape=jax.ShapeDtypeStruct((pieces.shape[1], units), jnp.bfloat16),
        interpret=INTERPRET, compiler_params=pltpu.CompilerParams(vmem_limit_bytes=16 << 20), in_specs=[VM], out_specs=VM,
        name="activate",
    )(pieces)


def on_device(tokens, source, gain, gate_weight, up_weight, down_weight):
    ny, nc, nh, nl, nx = (lax.axis_size(a) for a in ("y", "c", "h", "l", "x"))
    share, depth = tokens.shape
    sizes = (ny, nc, nh, nl, nx, share)
    units = gate_weight.shape[1]
    gathered = copied_to_all(copied_to_all(tokens, "h"), NEAR)
    operands = (source[:, None], gathered, gain[None, :], gate_weight.T, up_weight.T)
    given = products(sizes, True, jnp.bfloat16, *operands)
    taken = lax.ppermute(given, "c", [(0, 1), (1, 0)])
    own = products(sizes, False, jnp.float32, *operands)
    both = (own + taken.astype(jnp.float32)).astype(jnp.bfloat16)
    pieces = swapped(both.reshape(ny, -1, both.shape[1]), "y")
    hidden = lax.all_gather(activate(pieces, units), ("y", "c"), axis=0, tiled=True)
    mixed = jnp.dot(hidden, down_weight, preferred_element_type=jnp.float32).astype(jnp.bfloat16)
    mixed = summed(swapped(mixed.reshape(nl * nx, -1, depth), NEAR))
    return summed(swapped(mixed.reshape(nh, share, depth), "h"))


def solution(mesh):
    row, col = mesh.shape["row"], mesh.shape["col"]
    shape = (row // 2, 2, col // (L * X), L, X)
    finer = Mesh(mesh.devices.reshape(shape), ("y", "c", "h", "l", "x"))
    rows, cols = ("y", "c"), ("h", "l", "x")
    placed = (P(cols, rows), P(), P(rows), P(rows, cols), P(rows, cols), P(cols, rows))
    return jax.shard_map(
        on_device, mesh=finer, in_specs=placed, out_specs=P(cols, rows), check_vma=False
    )
```

```python
import functools

import jax
import jax.numpy as jnp
from jax import lax
from jax.experimental import pallas as pl
from jax.experimental.pallas import tpu as pltpu
from jax.sharding import Mesh
from jax.sharding import PartitionSpec as P

WIDTH = 8192
X, L, CHUNKS = 4, 2, 2
VM = pl.BlockSpec(memory_space=pltpu.VMEM)
INTERPRET = False
NEAR = ("l", "x")
NT = (((1,), (1,)), ((), ()))


def swapped(value, axis):
    return lax.all_to_all(value, axis, split_axis=0, concat_axis=0, tiled=True)


def copied_to_all(value, axis):
    copies = jnp.broadcast_to(value, (lax.axis_size(axis), *value.shape))
    return swapped(copies, axis).reshape(-1, *value.shape[1:])


def summed(pieces):
    return jnp.sum(pieces.astype(jnp.float32), axis=0).astype(jnp.bfloat16)


def products_kernel(sizes, other, source_ref, gathered_ref, gain_ref, gate_ref, up_ref, out_ref, pick_ref, weight_ref):
    ny, nc, nh, nl, nx, share = sizes

    def place(n):
        return (n % nh * nl + n // (nh * nx)) * nx + n // nh % nx

    total = gathered_ref.shape[0]
    units, half = gate_ref.shape[0], weight_ref.shape[0]
    block = total // (ny * nc * CHUNKS)
    part = nh // CHUNKS
    core = lax.axis_index("c")
    wanted = nc - 1 - core if other else core
    row = lax.broadcasted_iota(jnp.int32, (share, total), 1)
    token = place(row // share) * share + row % share
    for at in range(0, total // nc, share):
        chunk, y, k = at // (ny * block), at // block % ny, at % block // share
        starts = []
        for c in range(nc):
            n = (y * nc + c) * block // share + k
            starts.append(place(n // part * nh + chunk * part + n % part) * share)
        start = pl.multiple_of(jnp.where(wanted == 0, starts[0], starts[1]), share)
        ids = source_ref[pl.ds(start, share), :]
        pick_ref[at : at + share, :] = jnp.where(ids == token, 1.0, 0.0).astype(jnp.bfloat16)
    merged = jnp.dot(pick_ref[...], gathered_ref[...], preferred_element_type=jnp.float32)
    squares = jnp.sum(merged * merged, axis=1, keepdims=True)
    weighted = (merged * gain_ref[...]).astype(jnp.bfloat16)
    weight_ref[units:, :] = jnp.zeros((half - units, weight_ref.shape[1]), jnp.bfloat16)
    weight_ref[:units, :] = gate_ref[...]
    gate = lax.dot_general(weighted, weight_ref[...], NT, preferred_element_type=jnp.float32)
    lane = lax.broadcasted_iota(jnp.int32, gate.shape, 1)
    out_ref[:, :half] = jnp.where(lane == units, squares, gate).astype(out_ref.dtype)
    weight_ref[:units, :] = up_ref[...]
    up = lax.dot_general(weighted, weight_ref[...], NT, preferred_element_type=jnp.float32)
    out_ref[:, half:] = up.astype(out_ref.dtype)


def products(sizes, other, kind, source, gathered, gain, gate_weight, up_weight):
    units, depth = gate_weight.shape
    half = -(-(units + 1) // 128) * 128
    kept = gathered.shape[0] // sizes[1]
    return pl.pallas_call(
        functools.partial(products_kernel, sizes, other),
        out_shape=jax.ShapeDtypeStruct((kept, 2 * half), kind),
        scratch_shapes=[
            pltpu.VMEM((kept, gathered.shape[0]), jnp.bfloat16),
            pltpu.VMEM((half, depth), jnp.bfloat16),
        ],
        interpret=INTERPRET, compiler_params=pltpu.CompilerParams(vmem_limit_bytes=16 << 20), in_specs=[VM] * 5, out_specs=VM,
        name="products_other" if other else "products_own",
    )(source, gathered, gain, gate_weight, up_weight)


def activate_kernel(units, pieces_ref, out_ref):
    total = jnp.sum(pieces_ref[...].astype(jnp.float32), axis=0)
    half = total.shape[1] // 2
    gate, up = total[:, :half], total[:, half:]
    scale = lax.rsqrt(gate[:, units : units + 1] / WIDTH + 1e-6)
    gate, up = scale * gate[:, :units], scale * up[:, :units]
    out_ref[...] = (gate / (1.0 + jnp.exp(-gate)) * up).astype(jnp.bfloat16)


def activate(pieces, units):
    return pl.pallas_call(
        functools.partial(activate_kernel, units),
        out_shape=jax.ShapeDtypeStruct((pieces.shape[1], units), jnp.bfloat16),
        interpret=INTERPRET, compiler_params=pltpu.CompilerParams(vmem_limit_bytes=16 << 20), in_specs=[VM], out_specs=VM,
        name="activate",
    )(pieces)


def on_device(tokens, source, gain, gate_weight, up_weight, down_weight):
    ny, nc, nh, nl, nx = (lax.axis_size(a) for a in ("y", "c", "h", "l", "x"))
    share, depth = tokens.shape
    sizes = (ny, nc, nh, nl, nx, share)
    units = gate_weight.shape[1]
    gathered = copied_to_all(copied_to_all(tokens, "h"), NEAR)
    operands = (source[:, None], gathered, gain[None, :], gate_weight.T, up_weight.T)
    given = products(sizes, True, jnp.bfloat16, *operands)
    taken = lax.ppermute(given, "c", [(0, 1), (1, 0)])
    own = products(sizes, False, jnp.float32, *operands)
    both = (own + taken.astype(jnp.float32)).astype(jnp.bfloat16)
    pieces = both.reshape(CHUNKS, ny, -1, both.shape[1])
    pieces = [swapped(pieces[k], "y") for k in range(CHUNKS)]
    sums = []
    for piece in pieces:
        hidden = lax.all_gather(activate(piece, units), ("y", "c"), axis=0, tiled=True)
        mixed = jnp.dot(hidden, down_weight, preferred_element_type=jnp.float32).astype(jnp.bfloat16)
        sums.append(summed(swapped(mixed.reshape(nl * nx, -1, depth), NEAR)))
    mixed = jnp.concatenate(sums, axis=0)
    return summed(swapped(mixed.reshape(nh, share, depth), "h"))


def solution(mesh):
    row, col = mesh.shape["row"], mesh.shape["col"]
    shape = (row // 2, 2, col // (L * X), L, X)
    finer = Mesh(mesh.devices.reshape(shape), ("y", "c", "h", "l", "x"))
    rows, cols = ("y", "c"), ("h", "l", "x")
    placed = (P(cols, rows), P(), P(rows), P(rows, cols), P(rows, cols), P(cols, rows))
    return jax.shard_map(
        on_device, mesh=finer, in_specs=placed, out_specs=P(cols, rows), check_vma=False
    )
```

```python
import functools

import jax
import jax.numpy as jnp
from jax import lax
from jax.experimental import pallas as pl
from jax.experimental.pallas import tpu as pltpu
from jax.sharding import Mesh
from jax.sharding import PartitionSpec as P

WIDTH = 8192
X, L = 4, 2
LANES, FOLD = 128, 4
VM = pl.BlockSpec(memory_space=pltpu.VMEM)
INTERPRET = False
NEAR = ("l", "x")
NT = (((1,), (1,)), ((), ()))


def swapped(value, axis):
    return lax.all_to_all(value, axis, split_axis=0, concat_axis=0, tiled=True)


def copied_to_all(value, axis):
    copies = jnp.broadcast_to(value, (lax.axis_size(axis), *value.shape))
    return swapped(copies, axis).reshape(-1, *value.shape[1:])


def summed(pieces):
    return jnp.sum(pieces.astype(jnp.float32), axis=0).astype(jnp.bfloat16)


def products_kernel(sizes, other, source_ref, gathered_ref, gain_ref, gate_ref, up_ref, out_ref, pick_ref, weight_ref):
    ny, nc, nh, nl, nx, share = sizes

    def place(n):
        return (n % nh * nl + n // (nh * nx)) * nx + n // nh % nx

    total = gathered_ref.shape[0]
    units, half = gate_ref.shape[0], weight_ref.shape[0]
    block = total // (ny * nc)
    core = lax.axis_index("c")
    wanted = nc - 1 - core if other else core
    row = lax.broadcasted_iota(jnp.int32, (share, total), 1)
    token = place(row // share) * share + row % share
    for y in range(ny):
        for k in range(block // share):
            starts = [place((y * nc + c) * block // share + k) * share for c in range(nc)]
            start = pl.multiple_of(jnp.where(wanted == 0, starts[0], starts[1]), share)
            ids = source_ref[pl.ds(start, share), :]
            at = y * block + k * share
            pick_ref[at : at + share, :] = jnp.where(ids == token, 1.0, 0.0).astype(jnp.bfloat16)
    merged = jnp.dot(pick_ref[...], gathered_ref[...], preferred_element_type=jnp.float32)
    squares = jnp.sum(merged * merged, axis=1, keepdims=True)
    weighted = (merged * gain_ref[...]).astype(jnp.bfloat16)
    weight_ref[units:, :] = jnp.zeros((half - units, weight_ref.shape[1]), jnp.bfloat16)
    weight_ref[:units, :] = gate_ref[...]
    gate = lax.dot_general(weighted, weight_ref[...], NT, preferred_element_type=jnp.float32)
    weight_ref[:units, :] = up_ref[...]
    up = lax.dot_general(weighted, weight_ref[...], NT, preferred_element_type=jnp.float32)
    full, tail = units // LANES, units % LANES
    over = 2 * tail - LANES
    rolled = pltpu.roll(up[:, full * LANES :], tail, 1)
    lane = lax.broadcasted_iota(jnp.int32, rolled.shape, 1)
    shared = jnp.where(lane < tail, gate[:, full * LANES :], rolled)
    rest = jnp.where(lane < over, rolled, jnp.where(lane == over, squares, 0.0))
    tiles = [v[:, t * LANES : (t + 1) * LANES] for v in (gate, up) for t in range(full)] + [shared]
    quarter = block // FOLD
    for y in range(ny):
        for t, tile in enumerate(tiles):
            out_ref[y, t * block : (t + 1) * block, :] = tile[y * block : (y + 1) * block].astype(out_ref.dtype)
        folded = rest[y * block : y * block + quarter]
        for k in range(1, FOLD):
            at = y * block + k * quarter
            folded += pltpu.roll(rest[at : at + quarter], k * LANES // FOLD, 1)
        out_ref[y, len(tiles) * block :, :] = folded.astype(out_ref.dtype)


def products(sizes, other, kind, source, gathered, gain, gate_weight, up_weight):
    units, depth = gate_weight.shape
    full, tail = units // LANES, units % LANES
    assert LANES <= 2 * tail < LANES + LANES // FOLD
    ny, nc = sizes[:2]
    kept = gathered.shape[0] // nc
    rows = kept // ny * (2 * full + 1) + kept // ny // FOLD
    return pl.pallas_call(
        functools.partial(products_kernel, sizes, other),
        out_shape=jax.ShapeDtypeStruct((ny, rows, LANES), kind),
        in_specs=[VM] * 5,
        out_specs=VM,
        scratch_shapes=[
            pltpu.VMEM((kept, gathered.shape[0]), jnp.bfloat16),
            pltpu.VMEM(((full + 1) * LANES, depth), jnp.bfloat16),
        ],
        interpret=INTERPRET,
        compiler_params=pltpu.CompilerParams(vmem_limit_bytes=16 << 20),
        name="products_other" if other else "products_own",
    )(source, gathered, gain, gate_weight, up_weight)


def activate_kernel(units, pieces_ref, out_ref):
    total = jnp.sum(pieces_ref[...].astype(jnp.float32), axis=0)
    full, tail = units // LANES, units % LANES
    block = out_ref.shape[0]
    tiles = [total[t * block : (t + 1) * block] for t in range(2 * full + 1)]
    folded = total[(2 * full + 1) * block :]
    parts = [folded] + [pltpu.roll(folded, LANES - k * LANES // FOLD, 1) for k in range(1, FOLD)]
    rest = jnp.concatenate(parts, axis=0)
    over = 2 * tail - LANES
    scale = lax.rsqrt(rest[:, over : over + 1] / WIDTH + 1e-6)
    shared = tiles[2 * full]
    lane = lax.broadcasted_iota(jnp.int32, shared.shape, 1)
    last = pltpu.roll(jnp.where(lane < tail, rest, shared), LANES - tail, 1)
    gates, ups = tiles[:full] + [shared], tiles[full : 2 * full] + [last]
    for t in range(full + 1):
        gate, up = scale * gates[t], scale * ups[t]
        value = (gate / (1.0 + jnp.exp(-gate)) * up).astype(jnp.bfloat16)
        width = LANES if t < full else tail
        out_ref[:, t * LANES : t * LANES + width] = value[:, :width]


def activate(pieces, units, share):
    return pl.pallas_call(
        functools.partial(activate_kernel, units),
        out_shape=jax.ShapeDtypeStruct((share, units), jnp.bfloat16),
        in_specs=[VM],
        out_specs=VM,
        interpret=INTERPRET,
        compiler_params=pltpu.CompilerParams(vmem_limit_bytes=16 << 20),
        name="activate",
    )(pieces)


def on_device(tokens, source, gain, gate_weight, up_weight, down_weight):
    ny, nc, nh, nl, nx = (lax.axis_size(a) for a in ("y", "c", "h", "l", "x"))
    share, depth = tokens.shape
    sizes = (ny, nc, nh, nl, nx, share)
    units = gate_weight.shape[1]
    gathered = copied_to_all(copied_to_all(tokens, "h"), NEAR)
    operands = (source[:, None], gathered, gain[None, :], gate_weight.T, up_weight.T)
    given = products(sizes, True, jnp.bfloat16, *operands)
    taken = lax.ppermute(given, "c", [(0, 1), (1, 0)])
    own = products(sizes, False, jnp.float32, *operands)
    both = (own + taken.astype(jnp.float32)).astype(jnp.bfloat16)
    pieces = swapped(both, "y")
    hidden = lax.all_gather(activate(pieces, units, gathered.shape[0] // (ny * nc)), ("y", "c"), axis=0, tiled=True)
    mixed = jnp.dot(hidden, down_weight, preferred_element_type=jnp.float32).astype(jnp.bfloat16)
    mixed = summed(swapped(mixed.reshape(nl * nx, -1, depth), NEAR))
    return summed(swapped(mixed.reshape(nh, share, depth), "h"))


def solution(mesh):
    row, col = mesh.shape["row"], mesh.shape["col"]
    shape = (row // 2, 2, col // (L * X), L, X)
    finer = Mesh(mesh.devices.reshape(shape), ("y", "c", "h", "l", "x"))
    rows, cols = ("y", "c"), ("h", "l", "x")
    placed = (P(cols, rows), P(), P(rows), P(rows, cols), P(rows, cols), P(cols, rows))
    return jax.shard_map(
        on_device, mesh=finer, in_specs=placed, out_specs=P(cols, rows), check_vma=False
    )
```

```python
import functools

import jax
import jax.numpy as jnp
from jax import lax
from jax.experimental import pallas as pl
from jax.experimental.pallas import tpu as pltpu
from jax.sharding import Mesh
from jax.sharding import PartitionSpec as P

WIDTH = 8192
X, L = 4, 2
LANES, FOLD = 128, 4
VM = pl.BlockSpec(memory_space=pltpu.VMEM)
INTERPRET = False
NEAR = ("l", "x")
NT = (((1,), (1,)), ((), ()))


def swapped(value, axis):
    return lax.all_to_all(value, axis, split_axis=0, concat_axis=0, tiled=True)


def copied_to_all(value, axis):
    copies = jnp.broadcast_to(value, (lax.axis_size(axis), *value.shape))
    return swapped(copies, axis).reshape(-1, *value.shape[1:])


def summed(pieces):
    return jnp.sum(pieces.astype(jnp.float32), axis=0).astype(jnp.bfloat16)


def pick_kernel(sizes, source_ref, out_ref):
    ny, nc, nh, nl, nx, share = sizes
    total, part = out_ref.shape[0], share // nc

    def place(h, near):
        return ((h * nl + near // nx) * nx + near % nx) * share

    row = lax.broadcasted_iota(jnp.int32, (share, total), 1)
    block = total // (ny * nc)
    kept = row // (nc * block) * block + row % block
    token = place(kept // part % nh, kept // (part * nh)) + row // block % nc * part + kept % part
    for at in range(0, total, share):
        n = at // share
        start = place(n % nh, n // nh)
        ids = source_ref[start : start + share, :]
        out_ref[at : at + share, :] = jnp.where(ids == token, 1.0, 0.0).astype(jnp.bfloat16)


def pick_rows(sizes, source):
    total = source.shape[0]
    return pl.pallas_call(
        functools.partial(pick_kernel, sizes),
        out_shape=jax.ShapeDtypeStruct((total, total), jnp.bfloat16),
        in_specs=[VM],
        out_specs=VM,
        interpret=INTERPRET,
        compiler_params=pltpu.CompilerParams(vmem_limit_bytes=16 << 20),
        name="pick_rows",
    )(source[:, None])


def mixed_kernel(pick_ref, hidden_ref, down_ref, out_ref):
    chosen = jnp.dot(pick_ref[...], hidden_ref[...], preferred_element_type=jnp.float32)
    chosen = chosen.astype(jnp.bfloat16)
    out = jnp.dot(chosen, down_ref[...], preferred_element_type=jnp.float32)
    out_ref[...] = out.astype(jnp.bfloat16)


def mixed_rows(pick, hidden, down_weight):
    return pl.pallas_call(
        mixed_kernel,
        out_shape=jax.ShapeDtypeStruct((pick.shape[0], down_weight.shape[1]), jnp.bfloat16),
        in_specs=[VM] * 3,
        out_specs=VM,
        interpret=INTERPRET,
        compiler_params=pltpu.CompilerParams(vmem_limit_bytes=24 << 20),
        name="mixed_rows",
    )(pick, hidden, down_weight)


def products_kernel(gathered_ref, *refs):
    sides, (out_ref, weight_ref) = (refs[:3], refs[3:6]), refs[6:]
    ny, depth, units = out_ref.shape[0], gathered_ref.shape[3], refs[1].shape[0]
    kept = gathered_ref.shape[0] * gathered_ref.shape[2]
    block = kept // ny
    weight_ref[units:, :] = jnp.zeros((weight_ref.shape[0] - units, depth), jnp.bfloat16)
    core = lax.axis_index("c")
    squares, gate, up = 0.0, 0.0, 0.0
    for side, (gain_ref, gate_ref, up_ref) in zip((core, 1 - core), sides):
        merged = gathered_ref[:, pl.ds(side, 1)].astype(jnp.float32).reshape(kept, depth)
        squares += jnp.sum(merged * merged, axis=1, keepdims=True)
        weighted = (merged * gain_ref[...]).astype(jnp.bfloat16)
        weight_ref[:units, :] = gate_ref[...]
        gate += lax.dot_general(weighted, weight_ref[...], NT, preferred_element_type=jnp.float32)
        weight_ref[:units, :] = up_ref[...]
        up += lax.dot_general(weighted, weight_ref[...], NT, preferred_element_type=jnp.float32)
    full, tail = units // LANES, units % LANES
    over = 2 * tail - LANES
    rolled = pltpu.roll(up[:, full * LANES :], tail, 1)
    lane = lax.broadcasted_iota(jnp.int32, rolled.shape, 1)
    shared = jnp.where(lane < tail, gate[:, full * LANES :], rolled)
    rest = jnp.where(lane < over, rolled, jnp.where(lane == over, squares, 0.0))
    tiles = [v[:, t * LANES : (t + 1) * LANES] for v in (gate, up) for t in range(full)] + [shared]
    quarter = block // FOLD
    for y in range(ny):
        for t, tile in enumerate(tiles):
            out_ref[y, t * block : (t + 1) * block, :] = tile[y * block : (y + 1) * block].astype(out_ref.dtype)
        folded = rest[y * block : y * block + quarter]
        for k in range(1, FOLD):
            at = y * block + k * quarter
            folded += pltpu.roll(rest[at : at + quarter], k * LANES // FOLD, 1)
        out_ref[y, len(tiles) * block :, :] = folded.astype(out_ref.dtype)


def products(ny, gathered, *sides):
    units, depth = sides[1].shape
    full, tail = units // LANES, units % LANES
    assert LANES <= 2 * tail < LANES + LANES // FOLD
    block = gathered.shape[0] * gathered.shape[2] // ny
    rows = block * (2 * full + 1) + block // FOLD
    return pl.pallas_call(
        products_kernel,
        out_shape=jax.ShapeDtypeStruct((ny, rows, LANES), jnp.bfloat16),
        in_specs=[VM] * 7,
        out_specs=VM,
        scratch_shapes=[pltpu.VMEM(((full + 1) * LANES, depth), jnp.bfloat16)],
        interpret=INTERPRET,
        compiler_params=pltpu.CompilerParams(vmem_limit_bytes=24 << 20),
        name="products",
    )(gathered, *sides)


def activate_kernel(units, pieces_ref, out_ref):
    total = jnp.sum(pieces_ref[...].astype(jnp.float32), axis=0)
    full, tail = units // LANES, units % LANES
    block = out_ref.shape[0]
    tiles = [total[t * block : (t + 1) * block] for t in range(2 * full + 1)]
    folded = total[(2 * full + 1) * block :]
    parts = [folded] + [pltpu.roll(folded, LANES - k * LANES // FOLD, 1) for k in range(1, FOLD)]
    rest = jnp.concatenate(parts, axis=0)
    over = 2 * tail - LANES
    scale = lax.rsqrt(rest[:, over : over + 1] / WIDTH + 1e-6)
    shared = tiles[2 * full]
    lane = lax.broadcasted_iota(jnp.int32, shared.shape, 1)
    last = pltpu.roll(jnp.where(lane < tail, rest, shared), LANES - tail, 1)
    gates, ups = tiles[:full] + [shared], tiles[full : 2 * full] + [last]
    for t in range(full + 1):
        gate, up = scale * gates[t], scale * ups[t]
        value = (gate / (1.0 + jnp.exp(-gate)) * up).astype(jnp.bfloat16)
        width = LANES if t < full else tail
        out_ref[:, t * LANES : t * LANES + width] = value[:, :width]


def activate(pieces, units, share):
    return pl.pallas_call(
        functools.partial(activate_kernel, units),
        out_shape=jax.ShapeDtypeStruct((share, units), jnp.bfloat16),
        in_specs=[VM],
        out_specs=VM,
        interpret=INTERPRET,
        compiler_params=pltpu.CompilerParams(vmem_limit_bytes=16 << 20),
        name="activate",
    )(pieces)


def on_device(tokens, source, gain, gate_weight, up_weight, down_weight):
    ny, nc, nh, nl, nx = (lax.axis_size(a) for a in ("y", "c", "h", "l", "x"))
    share, depth = tokens.shape
    units, part = gate_weight.shape[1], share // nc
    sizes = (ny, nc, nh, nl, nx, share)
    halves = jnp.broadcast_to(tokens.reshape(nc, 1, part, depth), (nc, nh, part, depth))
    halves = swapped(halves.reshape(nc * nh, part, depth), ("c", "h")).reshape(-1, depth)
    gathered = copied_to_all(halves, NEAR).reshape(nl * nx, nc, nh * part, depth)
    own = (gain[None, :], gate_weight.T, up_weight.T)
    other = [lax.ppermute(v, "c", [(0, 1), (1, 0)]) for v in own]
    pieces = swapped(products(ny, gathered, *own, *other), "y")
    hidden = activate(pieces, units, nl * nx * nh * part // ny)
    hidden = lax.all_gather(hidden, ("y", "c"), axis=0, tiled=True)
    mixed = mixed_rows(pick_rows(sizes, source), hidden, down_weight)
    mixed = summed(swapped(mixed.reshape(nl * nx, -1, depth), NEAR))
    return summed(swapped(mixed.reshape(nh, share, depth), "h"))


def solution(mesh):
    row, col = mesh.shape["row"], mesh.shape["col"]
    shape = (row // 2, 2, col // (L * X), L, X)
    finer = Mesh(mesh.devices.reshape(shape), ("y", "c", "h", "l", "x"))
    rows, cols = ("y", "c"), ("h", "l", "x")
    placed = (P(cols, rows), P(), P(rows), P(rows, cols), P(rows, cols), P(cols, rows))
    return jax.shard_map(
        on_device, mesh=finer, in_specs=placed, out_specs=P(cols, rows), check_vma=False
    )
```

```python
import functools

import jax
import jax.numpy as jnp
from jax import lax
from jax.experimental import pallas as pl
from jax.experimental.pallas import tpu as pltpu
from jax.sharding import Mesh
from jax.sharding import PartitionSpec as P

WIDTH = 8192
X, L = 4, 2
LANES, FOLD = 128, 4
VM = pl.BlockSpec(memory_space=pltpu.VMEM)
INTERPRET = False
NEAR = ("l", "x")
NT = (((1,), (1,)), ((), ()))


def swapped(value, axis):
    return lax.all_to_all(value, axis, split_axis=0, concat_axis=0, tiled=True)


def copied_to_all(value, axis):
    copies = jnp.broadcast_to(value, (lax.axis_size(axis), *value.shape))
    return swapped(copies, axis).reshape(-1, *value.shape[1:])


def summed(pieces):
    return jnp.sum(pieces.astype(jnp.float32), axis=0).astype(jnp.bfloat16)


def pick_kernel(sizes, source_ref, out_ref):
    ny, nc, nh, nl, nx, share = sizes
    total, part = out_ref.shape[0], share // nc

    def place(h, near):
        return ((h * nl + near // nx) * nx + near % nx) * share

    row = lax.broadcasted_iota(jnp.int32, (share, total), 1)
    block = total // (ny * nc)
    kept = row // (nc * block) * block + row % block
    token = place(kept // part % nh, kept // (part * nh)) + row // block % nc * part + kept % part
    for at in range(0, total, share):
        n = at // share
        start = place(n % nh, n // nh)
        ids = source_ref[start : start + share, :]
        out_ref[at : at + share, :] = jnp.where(ids == token, 1.0, 0.0).astype(jnp.bfloat16)


def pick_rows(sizes, source):
    total = source.shape[0]
    return pl.pallas_call(
        functools.partial(pick_kernel, sizes),
        out_shape=jax.ShapeDtypeStruct((total, total), jnp.bfloat16),
        in_specs=[VM],
        out_specs=VM,
        interpret=INTERPRET,
        compiler_params=pltpu.CompilerParams(vmem_limit_bytes=16 << 20),
        name="pick_rows",
    )(source[:, None])


def mixed_kernel(pick_ref, hidden_ref, down_ref, out_ref):
    chosen = jnp.dot(pick_ref[...], hidden_ref[...], preferred_element_type=jnp.float32)
    chosen = chosen.astype(jnp.bfloat16)
    out = jnp.dot(chosen, down_ref[...], preferred_element_type=jnp.float32)
    out_ref[...] = out.astype(jnp.bfloat16)


def mixed_rows(pick, hidden, down_weight):
    return pl.pallas_call(
        mixed_kernel,
        out_shape=jax.ShapeDtypeStruct((pick.shape[0], down_weight.shape[1]), jnp.bfloat16),
        in_specs=[VM] * 3,
        out_specs=VM,
        interpret=INTERPRET,
        compiler_params=pltpu.CompilerParams(vmem_limit_bytes=24 << 20),
        name="mixed_rows",
    )(pick, hidden, down_weight)


def products_kernel(gathered_ref, *refs):
    sides, (out_ref, weight_ref) = (refs[:3], refs[3:6]), refs[6:]
    ny, depth, units = out_ref.shape[0], gathered_ref.shape[3], refs[1].shape[0]
    kept = gathered_ref.shape[0] * gathered_ref.shape[2]
    block = kept // ny
    weight_ref[units:, :] = jnp.zeros((weight_ref.shape[0] - units, depth), jnp.bfloat16)
    core = lax.axis_index("c")
    squares, gate, up = 0.0, 0.0, 0.0
    for side, (gain_ref, gate_ref, up_ref) in zip((core, 1 - core), sides):
        merged = gathered_ref[:, pl.ds(side, 1)].astype(jnp.float32).reshape(kept, depth)
        squares += jnp.sum(merged * merged, axis=1, keepdims=True)
        weighted = (merged * gain_ref[...]).astype(jnp.bfloat16)
        weight_ref[:units, :] = gate_ref[...]
        gate += lax.dot_general(weighted, weight_ref[...], NT, preferred_element_type=jnp.float32)
        weight_ref[:units, :] = up_ref[...]
        up += lax.dot_general(weighted, weight_ref[...], NT, preferred_element_type=jnp.float32)
    full, tail = units // LANES, units % LANES
    over = 2 * tail - LANES
    rolled = pltpu.roll(up[:, full * LANES :], tail, 1)
    lane = lax.broadcasted_iota(jnp.int32, rolled.shape, 1)
    shared = jnp.where(lane < tail, gate[:, full * LANES :], rolled)
    rest = jnp.where(lane < over, rolled, jnp.where(lane == over, squares, 0.0))
    tiles = [v[:, t * LANES : (t + 1) * LANES] for v in (gate, up) for t in range(full)] + [shared]
    quarter = block // FOLD
    for y in range(ny):
        for t, tile in enumerate(tiles):
            out_ref[y, t * block : (t + 1) * block, :] = tile[y * block : (y + 1) * block].astype(out_ref.dtype)
        folded = rest[y * block : y * block + quarter]
        for k in range(1, FOLD):
            at = y * block + k * quarter
            folded += pltpu.roll(rest[at : at + quarter], k * LANES // FOLD, 1)
        out_ref[y, len(tiles) * block :, :] = folded.astype(out_ref.dtype)


def products(ny, gathered, *sides):
    units, depth = sides[1].shape
    full, tail = units // LANES, units % LANES
    assert LANES <= 2 * tail < LANES + LANES // FOLD
    block = gathered.shape[0] * gathered.shape[2] // ny
    rows = block * (2 * full + 1) + block // FOLD
    return pl.pallas_call(
        products_kernel,
        out_shape=jax.ShapeDtypeStruct((ny, rows, LANES), jnp.bfloat16),
        in_specs=[VM] * 7,
        out_specs=VM,
        scratch_shapes=[pltpu.VMEM(((full + 1) * LANES, depth), jnp.bfloat16)],
        interpret=INTERPRET,
        compiler_params=pltpu.CompilerParams(vmem_limit_bytes=24 << 20),
        name="products",
    )(gathered, *sides)


def activate_kernel(units, pieces_ref, out_ref):
    total = jnp.sum(pieces_ref[...].astype(jnp.float32), axis=0)
    full, tail = units // LANES, units % LANES
    block = out_ref.shape[0]
    tiles = [total[t * block : (t + 1) * block] for t in range(2 * full + 1)]
    folded = total[(2 * full + 1) * block :]
    parts = [folded] + [pltpu.roll(folded, LANES - k * LANES // FOLD, 1) for k in range(1, FOLD)]
    rest = jnp.concatenate(parts, axis=0)
    over = 2 * tail - LANES
    scale = lax.rsqrt(rest[:, over : over + 1] / WIDTH + 1e-6)
    shared = tiles[2 * full]
    lane = lax.broadcasted_iota(jnp.int32, shared.shape, 1)
    last = pltpu.roll(jnp.where(lane < tail, rest, shared), LANES - tail, 1)
    gates, ups = tiles[:full] + [shared], tiles[full : 2 * full] + [last]
    for t in range(full + 1):
        gate, up = scale * gates[t], scale * ups[t]
        value = (gate / (1.0 + jnp.exp(-gate)) * up).astype(jnp.bfloat16)
        width = LANES if t < full else tail
        out_ref[:, t * LANES : t * LANES + width] = value[:, :width]


def activate(pieces, units, share):
    return pl.pallas_call(
        functools.partial(activate_kernel, units),
        out_shape=jax.ShapeDtypeStruct((share, units), jnp.bfloat16),
        in_specs=[VM],
        out_specs=VM,
        interpret=INTERPRET,
        compiler_params=pltpu.CompilerParams(vmem_limit_bytes=16 << 20),
        name="activate",
    )(pieces)


def on_device(tokens, source, gain, gate_weight, up_weight, down_weight):
    ny, nc, nh, nl, nx = (lax.axis_size(a) for a in ("y", "c", "h", "l", "x"))
    share, depth = tokens.shape
    units, part = gate_weight.shape[1], share // nc
    sizes = (ny, nc, nh, nl, nx, share)
    halves = jnp.broadcast_to(tokens.reshape(nc, 1, part, depth), (nc, nh, part, depth))
    halves = swapped(halves.reshape(nc * nh, part, depth), ("c", "h")).reshape(-1, depth)
    own = (gain[None, :], gate_weight.T, up_weight.T)
    other = [lax.ppermute(v, "c", [(0, 1), (1, 0)]) for v in own]
    early = (halves, pick_rows(sizes, source), other)
    halves, pick, other = lax.optimization_barrier(early)
    gathered = copied_to_all(halves, NEAR).reshape(nl * nx, nc, nh * part, depth)
    pieces = swapped(products(ny, gathered, *own, *other), "y")
    hidden = activate(pieces, units, nl * nx * nh * part // ny)
    hidden = lax.all_gather(hidden, ("y", "c"), axis=0, tiled=True)
    mixed = mixed_rows(pick, hidden, down_weight)
    mixed = summed(swapped(mixed.reshape(nl * nx, -1, depth), NEAR))
    return summed(swapped(mixed.reshape(nh, share, depth), "h"))


def solution(mesh):
    row, col = mesh.shape["row"], mesh.shape["col"]
    shape = (row // 2, 2, col // (L * X), L, X)
    finer = Mesh(mesh.devices.reshape(shape), ("y", "c", "h", "l", "x"))
    rows, cols = ("y", "c"), ("h", "l", "x")
    placed = (P(cols, rows), P(), P(rows), P(rows, cols), P(rows, cols), P(cols, rows))
    return jax.shard_map(
        on_device, mesh=finer, in_specs=placed, out_specs=P(cols, rows), check_vma=False
    )
```

```python
import functools

import jax
import jax.numpy as jnp
from jax import lax
from jax.experimental import pallas as pl
from jax.experimental.pallas import tpu as pltpu
from jax.sharding import Mesh
from jax.sharding import PartitionSpec as P

WIDTH = 8192
X, L = 4, 2
LANES, FOLD = 128, 4
VM = pl.BlockSpec(memory_space=pltpu.VMEM)
INTERPRET = False
NEAR = ("l", "x")
NT = (((1,), (1,)), ((), ()))


def swapped(value, axis):
    return lax.all_to_all(value, axis, split_axis=0, concat_axis=0, tiled=True)


def copied_to_all(value, axis):
    copies = jnp.broadcast_to(value, (lax.axis_size(axis), *value.shape))
    return swapped(copies, axis).reshape(-1, *value.shape[1:])


def summed(pieces):
    return jnp.sum(pieces.astype(jnp.float32), axis=0).astype(jnp.bfloat16)


def pick_kernel(sizes, source_ref, out_ref):
    ny, nc, nh, nl, nx, share = sizes
    total, part = out_ref.shape[0], share // nc

    def place(h, near):
        return ((h * nl + near // nx) * nx + near % nx) * share

    row = lax.broadcasted_iota(jnp.int32, (share, total), 1)
    block = total // (ny * nc)
    kept = row // (nc * block) * block + row % block
    token = place(kept // part % nh, kept // (part * nh)) + row // block % nc * part + kept % part
    for at in range(0, total, share):
        n = at // share
        start = place(n % nh, n // nh)
        ids = source_ref[start : start + share, :]
        out_ref[at : at + share, :] = jnp.where(ids == token, 1.0, 0.0).astype(jnp.bfloat16)


def pick_rows(sizes, source):
    total = source.shape[0]
    return pl.pallas_call(
        functools.partial(pick_kernel, sizes),
        out_shape=jax.ShapeDtypeStruct((total, total), jnp.bfloat16),
        in_specs=[VM],
        out_specs=VM,
        interpret=INTERPRET,
        compiler_params=pltpu.CompilerParams(vmem_limit_bytes=16 << 20),
        name="pick_rows",
    )(source[:, None])


def mixed_kernel(pick_ref, hidden_ref, down_ref, out_ref):
    chosen = jnp.dot(pick_ref[...], hidden_ref[...], preferred_element_type=jnp.float32)
    chosen = chosen.astype(jnp.bfloat16)
    out = jnp.dot(chosen, down_ref[...], preferred_element_type=jnp.float32)
    out_ref[...] = out.astype(jnp.bfloat16)


def mixed_rows(pick, hidden, down_weight):
    return pl.pallas_call(
        mixed_kernel,
        out_shape=jax.ShapeDtypeStruct((pick.shape[0], down_weight.shape[1]), jnp.bfloat16),
        in_specs=[VM] * 3,
        out_specs=VM,
        interpret=INTERPRET,
        compiler_params=pltpu.CompilerParams(vmem_limit_bytes=24 << 20),
        name="mixed_rows",
    )(pick, hidden, down_weight)


def products_kernel(gathered_ref, *refs):
    sides, (out_ref, row_ref, gate_all, up_all) = (refs[:3], refs[3:6]), refs[6:]
    ny, depth, units = out_ref.shape[0], gathered_ref.shape[3], refs[1].shape[0]
    kept = gathered_ref.shape[0] * gathered_ref.shape[2]
    block = kept // ny
    core = lax.axis_index("c")
    squares = 0.0
    for k, (gain_ref, gate_ref, up_ref) in enumerate(sides):
        at = k * depth
        side = core if k == 0 else 1 - core
        for weight_ref, all_ref in ((gate_ref, gate_all), (up_ref, up_all)):
            all_ref[units:, at : at + depth] = jnp.zeros((all_ref.shape[0] - units, depth), jnp.bfloat16)
            all_ref[:units, at : at + depth] = weight_ref[...]
        merged = gathered_ref[:, pl.ds(side, 1)].astype(jnp.float32).reshape(kept, depth)
        squares += jnp.sum(merged * merged, axis=1, keepdims=True)
        row_ref[:, at : at + depth] = (merged * gain_ref[...]).astype(jnp.bfloat16)
    gate = lax.dot_general(row_ref[...], gate_all[...], NT, preferred_element_type=jnp.float32)
    up = lax.dot_general(row_ref[...], up_all[...], NT, preferred_element_type=jnp.float32)
    full, tail = units // LANES, units % LANES
    over = 2 * tail - LANES
    rolled = pltpu.roll(up[:, full * LANES :], tail, 1)
    lane = lax.broadcasted_iota(jnp.int32, rolled.shape, 1)
    shared = jnp.where(lane < tail, gate[:, full * LANES :], rolled)
    rest = jnp.where(lane < over, rolled, jnp.where(lane == over, squares, 0.0))
    tiles = [v[:, t * LANES : (t + 1) * LANES] for v in (gate, up) for t in range(full)] + [shared]
    quarter = block // FOLD
    for y in range(ny):
        for t, tile in enumerate(tiles):
            out_ref[y, t * block : (t + 1) * block, :] = tile[y * block : (y + 1) * block].astype(out_ref.dtype)
        folded = rest[y * block : y * block + quarter]
        for k in range(1, FOLD):
            at = y * block + k * quarter
            folded += pltpu.roll(rest[at : at + quarter], k * LANES // FOLD, 1)
        out_ref[y, len(tiles) * block :, :] = folded.astype(out_ref.dtype)


def products(ny, gathered, *sides):
    units, depth = sides[1].shape
    full, tail = units // LANES, units % LANES
    assert LANES <= 2 * tail < LANES + LANES // FOLD
    block = gathered.shape[0] * gathered.shape[2] // ny
    rows = block * (2 * full + 1) + block // FOLD
    return pl.pallas_call(
        products_kernel,
        out_shape=jax.ShapeDtypeStruct((ny, rows, LANES), jnp.bfloat16),
        in_specs=[VM] * 7,
        out_specs=VM,
        scratch_shapes=[
            pltpu.VMEM((block * ny, 2 * depth), jnp.bfloat16),
            pltpu.VMEM(((full + 1) * LANES, 2 * depth), jnp.bfloat16),
            pltpu.VMEM(((full + 1) * LANES, 2 * depth), jnp.bfloat16),
        ],
        interpret=INTERPRET,
        compiler_params=pltpu.CompilerParams(vmem_limit_bytes=24 << 20),
        name="products",
    )(gathered, *sides)


def activate_kernel(units, pieces_ref, out_ref):
    total = jnp.sum(pieces_ref[...].astype(jnp.float32), axis=0)
    full, tail = units // LANES, units % LANES
    block = out_ref.shape[0]
    tiles = [total[t * block : (t + 1) * block] for t in range(2 * full + 1)]
    folded = total[(2 * full + 1) * block :]
    parts = [folded] + [pltpu.roll(folded, LANES - k * LANES // FOLD, 1) for k in range(1, FOLD)]
    rest = jnp.concatenate(parts, axis=0)
    over = 2 * tail - LANES
    scale = lax.rsqrt(rest[:, over : over + 1] / WIDTH + 1e-6)
    shared = tiles[2 * full]
    lane = lax.broadcasted_iota(jnp.int32, shared.shape, 1)
    last = pltpu.roll(jnp.where(lane < tail, rest, shared), LANES - tail, 1)
    gates, ups = tiles[:full] + [shared], tiles[full : 2 * full] + [last]
    for t in range(full + 1):
        gate, up = scale * gates[t], scale * ups[t]
        value = (gate / (1.0 + jnp.exp(-gate)) * up).astype(jnp.bfloat16)
        width = LANES if t < full else tail
        out_ref[:, t * LANES : t * LANES + width] = value[:, :width]


def activate(pieces, units, share):
    return pl.pallas_call(
        functools.partial(activate_kernel, units),
        out_shape=jax.ShapeDtypeStruct((share, units), jnp.bfloat16),
        in_specs=[VM],
        out_specs=VM,
        interpret=INTERPRET,
        compiler_params=pltpu.CompilerParams(vmem_limit_bytes=16 << 20),
        name="activate",
    )(pieces)


def on_device(tokens, source, gain, gate_weight, up_weight, down_weight):
    ny, nc, nh, nl, nx = (lax.axis_size(a) for a in ("y", "c", "h", "l", "x"))
    share, depth = tokens.shape
    units, part = gate_weight.shape[1], share // nc
    sizes = (ny, nc, nh, nl, nx, share)
    halves = jnp.broadcast_to(tokens.reshape(nc, 1, part, depth), (nc, nh, part, depth))
    halves = swapped(halves.reshape(nc * nh, part, depth), ("c", "h")).reshape(-1, depth)
    gathered = copied_to_all(halves, NEAR).reshape(nl * nx, nc, nh * part, depth)
    own = (gain[None, :], gate_weight.T, up_weight.T)
    other = [lax.ppermute(v, "c", [(0, 1), (1, 0)]) for v in own]
    pick = pick_rows(sizes, source)
    pieces = swapped(products(ny, gathered, *own, *other), "y")
    hidden = activate(pieces, units, nl * nx * nh * part // ny)
    hidden = lax.all_gather(hidden, ("y", "c"), axis=0, tiled=True)
    mixed = mixed_rows(pick, hidden, down_weight)
    mixed = summed(swapped(mixed.reshape(nl * nx, -1, depth), NEAR))
    return summed(swapped(mixed.reshape(nh, share, depth), "h"))


def solution(mesh):
    row, col = mesh.shape["row"], mesh.shape["col"]
    shape = (row // 2, 2, col // (L * X), L, X)
    finer = Mesh(mesh.devices.reshape(shape), ("y", "c", "h", "l", "x"))
    rows, cols = ("y", "c"), ("h", "l", "x")
    placed = (P(cols, rows), P(), P(rows), P(rows, cols), P(rows, cols), P(cols, rows))
    return jax.shard_map(
        on_device, mesh=finer, in_specs=placed, out_specs=P(cols, rows), check_vma=False
    )
```
